32 devices in a mesh: freq: 2 (over y), rcv: 4 (over z), src: 4 (over x, core).
Axes of the slice: x: 2, y: 2, z: 4, core: 2. Of those that a mesh axis runs over, the one named last changes fastest.
Arguments:
- traces: float32 [256, 2, 4096], P(('freq', 'src'), None, 'rcv'), parts along dimension 0, may hold values from -6 to 6
- moveout: float32 [2, 64, 16], P(None, 'freq'), parts along dimension 1, may hold values from -0.75 to 0.75
- trace_owner: int32 [8192], P(('freq', 'rcv')), parts along dimension 0, may hold values from 0 to 3, as said below
- trace_group: int32 [8192], P(('freq', 'rcv')), parts along dimension 0, may hold values from 0 to 127
- trace_table: int32 [8192], P(('freq', 'rcv')), parts along dimension 0, may hold values from 0 to 31
- aperture: float32 [2, 16384, 8192], P(None, ('freq', 'rcv'), 'src'), parts along dimension 1, may hold values from -0.046875 to 0.046875
- shaping: float32 [256, 2, 8192], P(('freq', 'src'), None, 'rcv'), parts along dimension 0, may hold values from -0.5 to 0.5
Outputs:
- demultiple: float32 [256, 2, 8192], P(('freq', 'src'), None, 'rcv'), parts along dimension 0
The draws below stay inside these ranges and needn't reach their ends.
There are 2 independent parts, one for each index of `freq`. The reference program is written for one: setup_inputs(seed, part) draws one part's arguments, and reference() takes and returns one part's arrays. A program takes and returns all parts, laid end to end along the dimension named above; each array names one. Nothing has to cross between parts.
Inputs may be any that keep to these rules, and one draw needn't show every extreme that they name: `trace_owner`: among the 1024 traces of each index of rcv (aligned blocks of the array), at most 512 name the same owner, and in every draw some owner is named by exactly 512 traces of every block.
All inputs are finite; a program needn't handle non-finite values.
Results may differ from the reference program's by a relative error of at most 0.0001.
Values sent between devices are 32-bit elements; how exact they have to be, the bound alone decides.
A program may use at most 128 MiB of HBM per device.

```python
import jax
import jax.numpy as jnp
from jax import lax

BINS = 8192
STENCIL = 16
TABLES = 32
ITERS = 2
TRACE_DEV = 1024
SHOTS = 128
TRACES = 4096
GROUPS = 128
CAPACITY = 512
N_RCV = 4


def draw_trace_owner(key, part):
    slot_total = N_RCV * CAPACITY
    owner_of_slot = jnp.arange(slot_total, dtype=jnp.int32) // CAPACITY
    owner_bias = jax.random.randint(jax.random.fold_in(key, 11), (N_RCV,), 0, 4096)
    forced_owner = jax.random.randint(jax.random.fold_in(key, 12), (), 0, N_RCV)

    def one_device(device_index):
        device_key = jax.random.fold_in(jax.random.fold_in(key, 13), device_index)
        slot_noise = jax.random.randint(jax.random.fold_in(device_key, 1), (slot_total,), 0, 4096)
        slot_score = slot_noise + owner_bias[owner_of_slot]
        slot_score = jnp.where(owner_of_slot == forced_owner, -1, slot_score)
        slot_score = (slot_score + 1) * slot_total + jnp.arange(slot_total, dtype=jnp.int32)
        chosen = jnp.argsort(slot_score)[:TRACE_DEV]
        shuffle = jax.random.permutation(jax.random.fold_in(device_key, 2), TRACE_DEV)
        return owner_of_slot[chosen][shuffle]
    return jax.vmap(one_device)(jnp.arange(N_RCV, dtype=jnp.int32)).reshape(-1).astype(jnp.int32)


def place_ends(drawn, own_key, smallest, largest):
    longest = drawn.shape.index(max(drawn.shape))
    spots = []
    for shift in (0, 1):
        where = [jax.random.randint(jax.random.fold_in(own_key, axis), (), 0, length) for axis, length in enumerate(drawn.shape)]
        where[longest] = (where[longest] + shift) % drawn.shape[longest]
        spots.append(tuple(where))
    return drawn.at[spots[0]].set(smallest).at[spots[1]].set(largest)


def block_scale(stream_key, extent, shards, least, largest):
    gain, own = 1.0, jax.random.fold_in(stream_key, 6)
    for dim, blocks in shards:
        heights = jnp.exp(jax.random.uniform(jax.random.fold_in(own, dim), (blocks,), jnp.float32, least / len(shards), largest / len(shards)))
        gain = gain * jnp.repeat(heights, extent[dim] // blocks).reshape([-1 if axis == dim else 1 for axis in range(len(extent))])
    return gain


def gaussian(rng, extent, scale, reach, shards=(), kind=jnp.bfloat16):
    drawn = jax.random.normal(rng, extent, jnp.float32) * scale
    if len(shards) > 0:
        drawn = block_scale(rng, extent, shards, -0.22, 0.18) * drawn
    return jnp.clip(drawn, min=-reach, max=reach).astype(kind)


def setup_inputs(seed: int = 0, part: int = 0) -> dict:
    key_of = jax.random.split(jax.random.key(seed), 8)
    own_keys = jax.random.split(jax.random.fold_in(key_of[7], part), 8)
    return {
        "traces": gaussian(own_keys[0], (SHOTS, 2, TRACES), 1.0, 6.0, ((0, 4), (2, 4)), jnp.float32),
        "moveout": gaussian(own_keys[1], (2, TABLES, STENCIL), 0.125, 0.75, (), jnp.float32),
        "trace_owner": draw_trace_owner(jax.random.fold_in(jax.random.fold_in(key_of[7], part), 71), part),
        "trace_group": place_ends(jax.random.randint(own_keys[3], (TRACES,), 0, GROUPS), jax.random.fold_in(own_keys[3], 1), 0, GROUPS - 1).astype(jnp.int32),
        "trace_table": place_ends(jax.random.randint(own_keys[4], (TRACES,), 0, TABLES), jax.random.fold_in(own_keys[4], 1), 0, TABLES - 1).astype(jnp.int32),
        "aperture": gaussian(own_keys[5], (2, BINS, BINS), (2 * BINS) ** -0.5, 0.046875, ((1, 4), (2, 4)), jnp.float32),
        "shaping": jnp.clip(jax.random.uniform(own_keys[6], (SHOTS, 2, BINS), jnp.float32, -0.5, 0.5) * block_scale(own_keys[6], (SHOTS, 2, BINS), ((0, 4), (2, 4)), -0.4, 0.0), -0.5, 0.5),
    }


def complex_join(partial_terms):
    return jnp.stack([partial_terms[:, 0, 0] - partial_terms[:, 1, 1], partial_terms[:, 0, 1] + partial_terms[:, 1, 0]], axis=1)


def complex_product(left_side, right_side):
    real_part = left_side[:, 0] * right_side[:, 0] - left_side[:, 1] * right_side[:, 1]
    imag_part = left_side[:, 0] * right_side[:, 1] + left_side[:, 1] * right_side[:, 0]
    return jnp.stack([real_part, imag_part], axis=1)


def reference(traces, moveout, trace_owner, trace_group, trace_table, aperture, shaping):
    highest = lax.Precision.HIGHEST
    bin_block = (trace_owner * GROUPS + trace_group).astype(jnp.int32)
    weights = moveout[:, trace_table, :]
    values = jnp.transpose(traces, (2, 1, 0))
    real_part = values[:, 0, None, :] * weights[0][:, :, None] - values[:, 1, None, :] * weights[1][:, :, None]
    real_sum = jax.ops.segment_sum(real_part, bin_block, num_segments=BINS // STENCIL)
    imag_part = values[:, 0, None, :] * weights[1][:, :, None] + values[:, 1, None, :] * weights[0][:, :, None]
    imag_sum = jax.ops.segment_sum(imag_part, bin_block, num_segments=BINS // STENCIL)
    binned = jnp.stack([real_sum, imag_sum], 0).reshape(2, BINS, SHOTS).transpose(2, 0, 1)
    panel_now = binned
    for sweep_index in range(ITERS):
        multiples = complex_join(jnp.einsum("sck,dik->scdi", panel_now, aperture, precision=highest))
        panel_now = binned - complex_product(shaping, multiples)
    return panel_now
```

```python
import functools

import jax
import jax.numpy as jnp
from jax import lax
from jax.experimental import pallas as pl
from jax.experimental.pallas import tpu as pltpu
from jax.sharding import PartitionSpec as P

ITERS = 2
MESH = pl.DeviceIdType.MESH
F32 = jnp.float32
BF16 = jnp.bfloat16
NT = (((1,), (1,)), ((), ()))


def split(value):
    high = value.astype(BF16)
    return high, (value - high.astype(F32)).astype(BF16)


def remote(src, dst, send_sem, recv_sem, where):
    return pltpu.make_async_remote_copy(
        src_ref=src,
        dst_ref=dst,
        send_sem=send_sem,
        recv_sem=recv_sem,
        device_id=where,
        device_id_type=MESH,
    )


def pieces(refs_shape, count):
    planes, rows = refs_shape[0], refs_shape[1]
    per = max(1, count // planes)
    step = rows // per
    return [(p, pl.ds(h * step, step)) for p in range(planes) for h in range(per)]


def gather_kernel(nz, ns, fold, plane, cuts, in_ref, out_ref, *scratch):
    if plane:
        held, zs, zr, ps, pr, ls = scratch
    else:
        held = out_ref
        zs, zr, ls = scratch
    z = lax.axis_index("rcv")
    c = lax.axis_index("src")
    width = in_ref.shape[-1]
    rows = in_ref.shape[1]

    barrier = pltpu.get_barrier_semaphore()
    for way in (1, -1):
        near = z + way

        @pl.when((near >= 0) & (near < nz))
        def _():
            pl.semaphore_signal(barrier, inc=1, device_id={"rcv": near}, device_id_type=MESH)

    if plane:
        for off in range(1, ns):
            pl.semaphore_signal(
                barrier, inc=1, device_id={"src": lax.rem(c + off, ns)}, device_id_type=MESH
            )
    peers = jnp.where(z > 0, 1, 0) + jnp.where(z < nz - 1, 1, 0)
    pl.semaphore_wait(barrier, peers + (ns - 1 if plane else 0))

    def along(src, block, lane, dist, q):
        way = 1 - 2 * lane
        cut = cuts[q]
        return remote(
            src.at[cut] if src is in_ref else src.at[(block,) + cut],
            held.at[(block,) + cut],
            zs.at[lane, dist, q],
            zr.at[lane, dist, q],
            {"rcv": z + way},
        )

    def place(who, f, q):
        p, r = cuts[q]
        return out_ref.at[
            p, pl.ds(pl.multiple_of(who * rows + r.start, 8), r.size), pl.ds(f * width, width)
        ]

    def across(src, block, q):
        f = block - (block // fold) * fold
        cut = cuts[q]
        return remote(
            src.at[cut] if src is in_ref else src.at[(block,) + cut],
            place(c, f, q),
            ps.at[block, q],
            pr.at[c, f, q],
            {"src": block // fold},
        )

    def local(src, block, q):
        f = block - (block // fold) * fold if plane else 0
        cut = cuts[q]
        there = place(c, f, q) if plane else held.at[(block,) + cut]
        here = src.at[cut] if src is in_ref else src.at[(block,) + cut]
        return pltpu.make_async_copy(here, there, ls.at[f, q])

    def hand_on(src, block, q):
        if not plane:
            return

        @pl.when(block // fold != c)
        def _():
            across(src, block, q).start()

        @pl.when(block // fold == c)
        def _():
            local(src, block, q).start()

    def has(lane):
        near = z + 1 - 2 * lane
        return (near >= 0) & (near < nz)

    for q in range(len(cuts)):
        for lane in (0, 1):

            @pl.when(has(lane))
            def _():
                along(in_ref, z, lane, 0, q).start()

        if plane:
            hand_on(in_ref, z, q)
        else:
            local(in_ref, z, q).start()

    def hop(dist, carry):
        for q in range(len(cuts)):
            for lane in (0, 1):
                block = z - dist * (1 - 2 * lane)

                @pl.when((block >= 0) & (block < nz))
                def _():
                    along(held, block, lane, dist - 1, q).wait_recv()

                    @pl.when(has(lane))
                    def _():
                        along(held, block, lane, dist, q).start()

                    hand_on(held, block, q)

        return carry

    lax.fori_loop(1, nz, hop, 0)

    def drain(dist, carry):
        for q in range(len(cuts)):
            for lane in (0, 1):
                block = z - dist * (1 - 2 * lane)

                @pl.when((block >= 0) & (block < nz) & has(lane))
                def _():
                    along(held, block, lane, dist, q).wait_send()

            if plane:

                @pl.when(dist // fold != c)
                def _():
                    across(held, dist, q).wait_send()

                @pl.when(dist // fold == c)
                def _():
                    local(held, dist, q).wait()

        return carry

    lax.fori_loop(0, nz, drain, 0)
    for q in range(len(cuts)):
        if not plane:
            local(in_ref, z, q).wait()
        else:
            for off in range(1, ns):
                who = lax.rem(c + off, ns)
                for f in range(fold):
                    remote(
                        place(who, f, q),
                        place(who, f, q),
                        ps.at[0, q],
                        pr.at[who, f, q],
                        {"src": who},
                    ).wait_recv()


def gather(value, nz, ns, plane, count, cid, name):
    planes, rows, width = value.shape
    fold = nz // ns
    cuts = pieces(value.shape, count)
    nq = len(cuts)
    dma = pltpu.SemaphoreType.DMA
    scratch = [dma((2, nz, nq)), dma((2, nz, nq))]
    if plane:
        out = jax.ShapeDtypeStruct((planes, ns * rows, fold * width), F32)
        scratch = [pltpu.VMEM((nz,) + value.shape, F32)] + scratch
        scratch += [dma((nz, nq)), dma((ns, fold, nq)), dma((fold, nq))]
    else:
        out = jax.ShapeDtypeStruct((nz,) + value.shape, F32)
        scratch += [dma((1, nq))]
    return pl.pallas_call(
        functools.partial(gather_kernel, nz, ns, fold, plane, cuts),
        out_shape=out,
        in_specs=[pl.BlockSpec(memory_space=pltpu.VMEM)],
        out_specs=pl.BlockSpec(memory_space=pltpu.VMEM),
        scratch_shapes=scratch,
        name=name,
        compiler_params=pltpu.CompilerParams(collective_id=cid, has_side_effects=True),
    )(value)


def bin_kernel(groups, tables, shots, wt_ref, x_ref, out_ref):
    stencil = wt_ref.shape[0] // 2
    rows = 2 * shots
    width = x_ref.shape[-1]
    me = lax.axis_index("rcv").astype(F32)
    owner = x_ref[0, 0, rows : rows + 1, :]
    group = x_ref[0, 0, rows + 1 : rows + 2, :]
    table = x_ref[0, 0, rows + 2 : rows + 3, :]
    table_ids = lax.broadcasted_iota(jnp.int32, (tables, width), 0).astype(F32)
    table_hot = (table_ids == table).astype(BF16)
    w = wt_ref[...]
    w0 = w.astype(BF16)
    rest = w - w0.astype(F32)
    w1 = rest.astype(BF16)
    w2 = (rest - w1.astype(F32)).astype(BF16)
    picked = sum(
        jnp.dot(part, table_hot, preferred_element_type=F32) for part in (w0, w1, w2)
    )
    group_ids = lax.broadcasted_iota(jnp.int32, (groups, width), 0).astype(F32)
    hot = ((group_ids == group) & (owner == me)).astype(BF16)
    real = x_ref[0, 0, 0:shots, :]
    imag = x_ref[0, 0, shots:rows, :]

    @pl.when(pl.program_id(0) == 0)
    def _():
        out_ref[...] = jnp.zeros_like(out_ref)

    for j in range(stencil):
        wr = picked[j : j + 1, :]
        wi = picked[stencil + j : stencil + j + 1, :]
        both = jnp.concatenate([real * wr - imag * wi, real * wi + imag * wr], axis=0)
        high, low = split(both)
        total = lax.dot_general(high, hot, NT, preferred_element_type=F32)
        total += lax.dot_general(low, hot, NT, preferred_element_type=F32)
        out_ref[j] += total


def bin_own(gathered, moveout, groups, shots):
    nz = gathered.shape[0]
    tables, stencil = moveout.shape[1:]
    weights = jnp.transpose(moveout, (0, 2, 1)).reshape(2 * stencil, tables)
    out = pl.pallas_call(
        functools.partial(bin_kernel, groups, tables, shots),
        grid=(nz,),
        out_shape=jax.ShapeDtypeStruct((stencil, 2 * shots, groups), F32),
        in_specs=[
            pl.BlockSpec(weights.shape, lambda i: (0, 0)),
            pl.BlockSpec((1,) + gathered.shape[1:], lambda i: (i, 0, 0, 0)),
        ],
        out_specs=pl.BlockSpec((stencil, 2 * shots, groups), lambda i: (0, 0, 0)),
        name="bin_own",
    )(weights, gathered)
    return jnp.transpose(out, (1, 2, 0)).reshape(2, shots, groups * stencil)


def multiply_kernel(ns, shots, steps, p_ref, a_ref, out_ref, high, low, sent, got, ss, rs):
    step = pl.program_id(0)
    c = lax.axis_index("src")
    half = ns * shots
    tile = a_ref.shape[1]

    @pl.when(step == 0)
    def _():
        barrier = pltpu.get_barrier_semaphore()
        for off in range(1, ns):
            pl.semaphore_signal(
                barrier, inc=1, device_id={"src": lax.rem(c + off, ns)}, device_id_type=MESH
            )
        for part in (0, 1):
            top, rest = split(p_ref[part])
            high[part * half : (part + 1) * half, :] = top
            low[part * half : (part + 1) * half, :] = rest
        pl.semaphore_wait(barrier, ns - 1)

    def times(part):
        top, rest = split(a_ref[part])
        total = lax.dot_general(high[...], top, NT, preferred_element_type=F32)
        total += lax.dot_general(low[...], top, NT, preferred_element_type=F32)
        total += lax.dot_general(high[...], rest, NT, preferred_element_type=F32)
        return total

    by_real = times(0)
    by_imag = times(1)
    sent[step, 0] = by_real[:half] - by_imag[half:]
    sent[step, 1] = by_imag[:half] + by_real[half:]

    def copy(at, off):
        who = lax.rem(c + off, ns)
        return remote(
            sent.at[at, :, pl.ds(pl.multiple_of(who * shots, 8), shots), :],
            got.at[off - 1, at],
            ss.at[off - 1, at],
            rs.at[off - 1, at],
            {"src": who},
        )

    for off in range(1, ns):
        copy(step, off).start()

    @pl.when(step == steps - 1)
    def _():
        mine = pl.ds(pl.multiple_of(c * shots, 8), shots)
        for at in range(steps):
            for off in range(1, ns):
                copy(at, off).wait_recv()
            total = sent[at, :, mine, :]
            for off in range(1, ns):
                total += got[off - 1, at]
            out_ref[:, :, at * tile : (at + 1) * tile] = total
        for at in range(steps):
            for off in range(1, ns):
                copy(at, off).wait_send()


def multiply(columns, aperture, ns, cid):
    _, half, depth = columns.shape
    outs = aperture.shape[1]
    shots = half // ns
    tile = min(outs, 256)
    steps = outs // tile
    dma = pltpu.SemaphoreType.DMA
    return pl.pallas_call(
        functools.partial(multiply_kernel, ns, shots, steps),
        grid=(steps,),
        out_shape=jax.ShapeDtypeStruct((2, shots, outs), F32),
        in_specs=[
            pl.BlockSpec(memory_space=pltpu.VMEM),
            pl.BlockSpec((2, tile, depth), lambda i: (0, i, 0)),
        ],
        out_specs=pl.BlockSpec(memory_space=pltpu.VMEM),
        scratch_shapes=[
            pltpu.VMEM((2 * half, depth), BF16),
            pltpu.VMEM((2 * half, depth), BF16),
            pltpu.VMEM((steps, 2, half, tile), F32),
            pltpu.VMEM((ns - 1, steps, 2, shots, tile), F32),
            dma((ns - 1, steps)),
            dma((ns - 1, steps)),
        ],
        name="multiply",
        compiler_params=pltpu.CompilerParams(
            collective_id=cid,
            has_side_effects=True,
            dimension_semantics=("arbitrary",),
            vmem_limit_bytes=56 << 20,
        ),
    )(columns, aperture)


def per_device(nz, ns, traces, moveout, owner, group, table, aperture, shaping):
    groups = aperture.shape[1] // moveout.shape[2]
    shots = traces.shape[0]
    width = traces.shape[2]
    codes = jnp.stack([owner, group, table]).astype(F32)
    codes = jnp.concatenate([codes, jnp.zeros((5, width), F32)])
    flat = jnp.transpose(traces, (1, 0, 2)).reshape(2 * shots, width)
    sources = gather(jnp.concatenate([flat, codes])[None], nz, ns, False, 3, 0, "gather_traces")
    binned = bin_own(sources, moveout, groups, shots)
    form = jnp.transpose(shaping, (1, 0, 2))
    panel = binned
    for sweep in range(ITERS):
        columns = gather(panel, nz, ns, True, 4, 1, "gather_panel")
        found = multiply(columns, aperture, ns, 2)
        panel = jnp.stack(
            [
                binned[0] - (form[0] * found[0] - form[1] * found[1]),
                binned[1] - (form[0] * found[1] + form[1] * found[0]),
            ]
        )
    return jnp.transpose(panel, (1, 0, 2))


def solution(mesh):
    nz, ns = mesh.shape["rcv"], mesh.shape["src"]
    in_specs = (
        P(("freq", "src"), None, "rcv"),
        P(None, "freq", None),
        P(("freq", "rcv")),
        P(("freq", "rcv")),
        P(("freq", "rcv")),
        P(None, ("freq", "rcv"), "src"),
        P(("freq", "src"), None, "rcv"),
    )
    out_specs = P(("freq", "src"), None, "rcv")
    return jax.shard_map(
        functools.partial(per_device, nz, ns),
        mesh=mesh,
        in_specs=in_specs,
        out_specs=out_specs,
        check_vma=False,
    )
```

```python
import functools

import jax
import jax.numpy as jnp
from jax import lax
from jax.experimental import pallas as pl
from jax.experimental.pallas import tpu as pltpu
from jax.sharding import PartitionSpec as P

ITERS = 2
MESH = pl.DeviceIdType.MESH
F32 = jnp.float32
BF16 = jnp.bfloat16
NT = (((1,), (1,)), ((), ()))


def split(value):
    high = value.astype(BF16)
    return high, (value - high.astype(F32)).astype(BF16)


def remote(src, dst, send_sem, recv_sem, where):
    return pltpu.make_async_remote_copy(
        src_ref=src,
        dst_ref=dst,
        send_sem=send_sem,
        recv_sem=recv_sem,
        device_id=where,
        device_id_type=MESH,
    )


def pieces(refs_shape, count):
    planes, rows = refs_shape[0], refs_shape[1]
    per = max(1, count // planes)
    step = rows // per
    return [(p, pl.ds(h * step, step)) for p in range(planes) for h in range(per)]


def gather_kernel(nz, ns, fold, plane, cuts, in_ref, out_ref, *scratch):
    if plane:
        held, zs, zr, ps, pr, ls = scratch
    else:
        held = out_ref
        zs, zr, ls = scratch
    z = lax.axis_index("rcv")
    c = lax.axis_index("src")
    width = in_ref.shape[-1]
    rows = in_ref.shape[1]

    barrier = pltpu.get_barrier_semaphore()
    for way in (1, -1):
        near = z + way

        @pl.when((near >= 0) & (near < nz))
        def _():
            pl.semaphore_signal(barrier, inc=1, device_id={"rcv": near}, device_id_type=MESH)

    if plane:
        for off in range(1, ns):
            pl.semaphore_signal(
                barrier, inc=1, device_id={"src": lax.rem(c + off, ns)}, device_id_type=MESH
            )
    peers = jnp.where(z > 0, 1, 0) + jnp.where(z < nz - 1, 1, 0)
    pl.semaphore_wait(barrier, peers + (ns - 1 if plane else 0))

    def along(src, block, lane, dist, q):
        way = 1 - 2 * lane
        cut = cuts[q]
        return remote(
            src.at[cut] if src is in_ref else src.at[(block,) + cut],
            held.at[(block,) + cut],
            zs.at[lane, dist, q],
            zr.at[lane, dist, q],
            {"rcv": z + way},
        )

    def place(who, f, q):
        p, r = cuts[q]
        return out_ref.at[
            p, pl.ds(pl.multiple_of(who * rows + r.start, 8), r.size), pl.ds(f * width, width)
        ]

    def across(src, block, q):
        f = block - (block // fold) * fold
        cut = cuts[q]
        return remote(
            src.at[cut] if src is in_ref else src.at[(block,) + cut],
            place(c, f, q),
            ps.at[block, q],
            pr.at[c, f, q],
            {"src": block // fold},
        )

    def local(src, block, q):
        f = block - (block // fold) * fold if plane else 0
        cut = cuts[q]
        there = place(c, f, q) if plane else held.at[(block,) + cut]
        here = src.at[cut] if src is in_ref else src.at[(block,) + cut]
        return pltpu.make_async_copy(here, there, ls.at[f, q])

    def hand_on(src, block, q):
        if not plane:
            return

        @pl.when(block // fold != c)
        def _():
            across(src, block, q).start()

        @pl.when(block // fold == c)
        def _():
            local(src, block, q).start()

    def has(lane):
        near = z + 1 - 2 * lane
        return (near >= 0) & (near < nz)

    for q in range(len(cuts)):
        for lane in (0, 1):

            @pl.when(has(lane))
            def _():
                along(in_ref, z, lane, 0, q).start()

        if plane:
            hand_on(in_ref, z, q)
        else:
            local(in_ref, z, q).start()

    def hop(dist, carry):
        for q in range(len(cuts)):
            for lane in (0, 1):
                block = z - dist * (1 - 2 * lane)

                @pl.when((block >= 0) & (block < nz))
                def _():
                    along(held, block, lane, dist - 1, q).wait_recv()

                    @pl.when(has(lane))
                    def _():
                        along(held, block, lane, dist, q).start()

                    hand_on(held, block, q)

        return carry

    lax.fori_loop(1, nz, hop, 0)

    def drain(dist, carry):
        for q in range(len(cuts)):
            for lane in (0, 1):
                block = z - dist * (1 - 2 * lane)

                @pl.when((block >= 0) & (block < nz) & has(lane))
                def _():
                    along(held, block, lane, dist, q).wait_send()

            if plane:

                @pl.when(dist // fold != c)
                def _():
                    across(held, dist, q).wait_send()

                @pl.when(dist // fold == c)
                def _():
                    local(held, dist, q).wait()

        return carry

    lax.fori_loop(0, nz, drain, 0)
    for q in range(len(cuts)):
        if not plane:
            local(in_ref, z, q).wait()
        else:
            for off in range(1, ns):
                who = lax.rem(c + off, ns)
                for f in range(fold):
                    remote(
                        place(who, f, q),
                        place(who, f, q),
                        ps.at[0, q],
                        pr.at[who, f, q],
                        {"src": who},
                    ).wait_recv()


def gather(value, nz, ns, plane, count, cid, name):
    planes, rows, width = value.shape
    fold = nz // ns
    cuts = pieces(value.shape, count)
    nq = len(cuts)
    dma = pltpu.SemaphoreType.DMA
    scratch = [dma((2, nz, nq)), dma((2, nz, nq))]
    if plane:
        out = jax.ShapeDtypeStruct((planes, ns * rows, fold * width), F32)
        scratch = [pltpu.VMEM((nz,) + value.shape, F32)] + scratch
        scratch += [dma((nz, nq)), dma((ns, fold, nq)), dma((fold, nq))]
    else:
        out = jax.ShapeDtypeStruct((nz,) + value.shape, F32)
        scratch += [dma((1, nq))]
    return pl.pallas_call(
        functools.partial(gather_kernel, nz, ns, fold, plane, cuts),
        out_shape=out,
        in_specs=[pl.BlockSpec(memory_space=pltpu.VMEM)],
        out_specs=pl.BlockSpec(memory_space=pltpu.VMEM),
        scratch_shapes=scratch,
        name=name,
        compiler_params=pltpu.CompilerParams(collective_id=cid, has_side_effects=True),
    )(value)


def bin_kernel(groups, tables, shots, wt_ref, x_ref, out_ref, terms, total, order):
    stencil = wt_ref.shape[0] // 2
    rows = 2 * shots
    width = x_ref.shape[-1]
    me = lax.axis_index("rcv").astype(F32)
    owner = x_ref[0, 0, rows : rows + 1, :]
    group = x_ref[0, 0, rows + 1 : rows + 2, :]
    table = x_ref[0, 0, rows + 2 : rows + 3, :]
    table_ids = lax.broadcasted_iota(jnp.int32, (tables, width), 0).astype(F32)
    table_hot = (table_ids == table).astype(BF16)
    w = wt_ref[...]
    w0 = w.astype(BF16)
    rest = w - w0.astype(F32)
    w1 = rest.astype(BF16)
    w2 = (rest - w1.astype(F32)).astype(BF16)
    picked = sum(
        jnp.dot(part, table_hot, preferred_element_type=F32) for part in (w0, w1, w2)
    )
    group_ids = lax.broadcasted_iota(jnp.int32, (groups, width), 0).astype(F32)
    hot = ((group_ids == group) & (owner == me)).astype(BF16)
    real = x_ref[0, 0, 0:shots, :]
    imag = x_ref[0, 0, shots:rows, :]

    for j in range(stencil):
        wr = picked[j : j + 1, :]
        wi = picked[stencil + j : stencil + j + 1, :]
        base = j * 2 * rows
        for part, both in enumerate((real * wr - imag * wi, real * wi + imag * wr)):
            high, low = split(both)
            at = base + part * shots
            terms[at : at + shots, :] = high
            terms[at + rows : at + rows + shots, :] = low

    found = lax.dot_general(terms[...], hot, NT, preferred_element_type=F32)
    found = found.reshape(stencil, 2, rows, groups)
    found = found[:, 0] + found[:, 1]

    @pl.when(pl.program_id(0) == 0)
    def _():
        total[...] = found

    @pl.when(pl.program_id(0) > 0)
    def _():
        total[...] += found

    @pl.when(pl.program_id(0) == pl.num_programs(0) - 1)
    def _():
        for j in range(stencil):
            order[:, j, :] = total[j].T
        out_ref[...] = order[...].reshape(groups * stencil, rows).T


def bin_own(gathered, moveout, groups, shots):
    nz = gathered.shape[0]
    tables, stencil = moveout.shape[1:]
    width = gathered.shape[-1]
    weights = jnp.transpose(moveout, (0, 2, 1)).reshape(2 * stencil, tables)
    out = pl.pallas_call(
        functools.partial(bin_kernel, groups, tables, shots),
        grid=(nz,),
        out_shape=jax.ShapeDtypeStruct((2 * shots, groups * stencil), F32),
        in_specs=[
            pl.BlockSpec(weights.shape, lambda i: (0, 0)),
            pl.BlockSpec((1,) + gathered.shape[1:], lambda i: (i, 0, 0, 0)),
        ],
        out_specs=pl.BlockSpec((2 * shots, groups * stencil), lambda i: (0, 0)),
        scratch_shapes=[
            pltpu.VMEM((stencil * 4 * shots, width), BF16),
            pltpu.VMEM((stencil, 2 * shots, groups), F32),
            pltpu.VMEM((groups, stencil, 2 * shots), F32),
        ],
        name="bin_own",
    )(weights, gathered)
    return out.reshape(2, shots, groups * stencil)


def multiply_kernel(
    ns, shots, steps, p_ref, a_ref, out_ref, high, low, mine, give, take, pass_on, got, s1, r1, s2, r2
):
    step = pl.program_id(0)
    c = lax.axis_index("src")
    core = lax.rem(c, 2)
    chip = c // 2
    chips = ns // 2
    half = ns * shots
    tile = a_ref.shape[1]

    @pl.when(step == 0)
    def _():
        barrier = pltpu.get_barrier_semaphore()
        pl.semaphore_signal(barrier, inc=1, device_id={"src": c + 1 - 2 * core}, device_id_type=MESH)
        for off in range(1, chips):
            who = 2 * lax.rem(chip + off, chips) + core
            pl.semaphore_signal(barrier, inc=1, device_id={"src": who}, device_id_type=MESH)
        for part in (0, 1):
            top, rest = split(p_ref[part])
            high[part * half : (part + 1) * half, :] = top
            low[part * half : (part + 1) * half, :] = rest
        pl.semaphore_wait(barrier, chips)

    def to_partner(at):
        return remote(give.at[at], take.at[at], s1.at[at], r1.at[at], {"src": c + 1 - 2 * core})

    def to_chip(at, off):
        who = 2 * lax.rem(chip + off, chips) + core
        return remote(
            pass_on.at[at, off - 1],
            got.at[at, off - 1],
            s2.at[at, off - 1],
            r2.at[at, off - 1],
            {"src": who},
        )

    def reduce_pair(at):
        to_partner(at).wait_recv()
        for off in range(1, chips):
            there = lax.rem(chip + off, chips)
            pass_on[at, off - 1] = mine[at, there] + take[at, there]
            to_chip(at, off).start()
        mine[at, chip] += take[at, chip]

    def times(part):
        top, rest = split(a_ref[part])
        total = lax.dot_general(high[...], top, NT, preferred_element_type=F32)
        total += lax.dot_general(low[...], top, NT, preferred_element_type=F32)
        total += lax.dot_general(high[...], rest, NT, preferred_element_type=F32)
        return total

    by_real = times(0)
    by_imag = times(1)
    both = (by_real[:half] - by_imag[half:], by_imag[:half] + by_real[half:])
    for part in (0, 1):
        for who in range(ns):
            value = both[part][who * shots : (who + 1) * shots]

            @pl.when(core == who % 2)
            def _():
                mine[step, who // 2, part] = value

            @pl.when(core != who % 2)
            def _():
                give[step, who // 2, part] = value

    to_partner(step).start()

    @pl.when(step > 0)
    def _():
        reduce_pair(step - 1)

    @pl.when(step == steps - 1)
    def _():
        reduce_pair(step)
        for at in range(steps):
            total = mine[at, chip]
            for off in range(1, chips):
                to_chip(at, off).wait_recv()
                total += got[at, off - 1]
            out_ref[:, :, at * tile : (at + 1) * tile] = total
        for at in range(steps):
            to_partner(at).wait_send()
            for off in range(1, chips):
                to_chip(at, off).wait_send()


def multiply(columns, aperture, ns, cid):
    _, half, depth = columns.shape
    outs = aperture.shape[1]
    shots = half // ns
    tile = min(outs, 256)
    steps = outs // tile
    chips = ns // 2
    dma = pltpu.SemaphoreType.DMA
    block = (2, shots, tile)
    return pl.pallas_call(
        functools.partial(multiply_kernel, ns, shots, steps),
        grid=(steps,),
        out_shape=jax.ShapeDtypeStruct((2, shots, outs), F32),
        in_specs=[
            pl.BlockSpec(memory_space=pltpu.VMEM),
            pl.BlockSpec((2, tile, depth), lambda i: (0, i, 0)),
        ],
        out_specs=pl.BlockSpec(memory_space=pltpu.VMEM),
        scratch_shapes=[
            pltpu.VMEM((2 * half, depth), BF16),
            pltpu.VMEM((2 * half, depth), BF16),
            pltpu.VMEM((steps, chips) + block, F32),
            pltpu.VMEM((steps, chips) + block, F32),
            pltpu.VMEM((steps, chips) + block, F32),
            pltpu.VMEM((steps, chips - 1) + block, F32),
            pltpu.VMEM((steps, chips - 1) + block, F32),
            dma((steps,)),
            dma((steps,)),
            dma((steps, chips - 1)),
            dma((steps, chips - 1)),
        ],
        name="multiply",
        compiler_params=pltpu.CompilerParams(
            collective_id=cid,
            has_side_effects=True,
            dimension_semantics=("arbitrary",),
            vmem_limit_bytes=56 << 20,
        ),
    )(columns, aperture)


def per_device(nz, ns, traces, moveout, owner, group, table, aperture, shaping):
    groups = aperture.shape[1] // moveout.shape[2]
    shots = traces.shape[0]
    width = traces.shape[2]
    codes = jnp.stack([owner, group, table]).astype(F32)
    codes = jnp.concatenate([codes, jnp.zeros((5, width), F32)])
    flat = jnp.transpose(traces, (1, 0, 2)).reshape(2 * shots, width)
    sources = gather(jnp.concatenate([flat, codes])[None], nz, ns, False, 3, 0, "gather_traces")
    binned = bin_own(sources, moveout, groups, shots)
    form = jnp.transpose(shaping, (1, 0, 2))
    panel = binned
    for sweep in range(ITERS):
        columns = gather(panel, nz, ns, True, 8, 1, "gather_panel")
        found = multiply(columns, aperture, ns, 2)
        panel = jnp.stack(
            [
                binned[0] - (form[0] * found[0] - form[1] * found[1]),
                binned[1] - (form[0] * found[1] + form[1] * found[0]),
            ]
        )
    return jnp.transpose(panel, (1, 0, 2))


def solution(mesh):
    nz, ns = mesh.shape["rcv"], mesh.shape["src"]
    in_specs = (
        P(("freq", "src"), None, "rcv"),
        P(None, "freq", None),
        P(("freq", "rcv")),
        P(("freq", "rcv")),
        P(("freq", "rcv")),
        P(None, ("freq", "rcv"), "src"),
        P(("freq", "src"), None, "rcv"),
    )
    out_specs = P(("freq", "src"), None, "rcv")
    return jax.shard_map(
        functools.partial(per_device, nz, ns),
        mesh=mesh,
        in_specs=in_specs,
        out_specs=out_specs,
        check_vma=False,
    )
```

```python
import functools

import jax
import jax.numpy as jnp
from jax import lax
from jax.experimental import pallas as pl
from jax.experimental.pallas import tpu as pltpu
from jax.sharding import PartitionSpec as P

ITERS = 2
MESH = pl.DeviceIdType.MESH
F32 = jnp.float32
BF16 = jnp.bfloat16
NT = (((1,), (1,)), ((), ()))


def split(value):
    high = value.astype(BF16)
    return high, (value - high.astype(F32)).astype(BF16)


def remote(src, dst, send_sem, recv_sem, where):
    return pltpu.make_async_remote_copy(
        src_ref=src,
        dst_ref=dst,
        send_sem=send_sem,
        recv_sem=recv_sem,
        device_id=where,
        device_id_type=MESH,
    )


def pieces(refs_shape, count):
    planes, rows = refs_shape[0], refs_shape[1]
    per = max(1, count // planes)
    step = rows // per
    return [(p, pl.ds(h * step, step)) for p in range(planes) for h in range(per)]


def gather_kernel(nz, ns, fold, plane, cuts, in_ref, out_ref, *scratch):
    if plane:
        held, zs, zr, ps, pr, ls = scratch
    else:
        held = out_ref
        zs, zr, ls = scratch
    z = lax.axis_index("rcv")
    c = lax.axis_index("src")
    width = in_ref.shape[-1]
    rows = in_ref.shape[1]

    barrier = pltpu.get_barrier_semaphore()
    for way in (1, -1):
        near = z + way

        @pl.when((near >= 0) & (near < nz))
        def _():
            pl.semaphore_signal(barrier, inc=1, device_id={"rcv": near}, device_id_type=MESH)

    if plane:
        for off in range(1, ns):
            pl.semaphore_signal(
                barrier, inc=1, device_id={"src": lax.rem(c + off, ns)}, device_id_type=MESH
            )
    peers = jnp.where(z > 0, 1, 0) + jnp.where(z < nz - 1, 1, 0)
    pl.semaphore_wait(barrier, peers + (ns - 1 if plane else 0))

    def along(src, block, lane, dist, q):
        way = 1 - 2 * lane
        cut = cuts[q]
        return remote(
            src.at[cut] if src is in_ref else src.at[(block,) + cut],
            held.at[(block,) + cut],
            zs.at[lane, dist, q],
            zr.at[lane, dist, q],
            {"rcv": z + way},
        )

    def place(who, f, q):
        p, r = cuts[q]
        return out_ref.at[
            p, pl.ds(pl.multiple_of(who * rows + r.start, 8), r.size), pl.ds(f * width, width)
        ]

    def across(src, block, q):
        f = block - (block // fold) * fold
        cut = cuts[q]
        return remote(
            src.at[cut] if src is in_ref else src.at[(block,) + cut],
            place(c, f, q),
            ps.at[block, q],
            pr.at[c, f, q],
            {"src": block // fold},
        )

    def local(src, block, q):
        f = block - (block // fold) * fold if plane else 0
        cut = cuts[q]
        there = place(c, f, q) if plane else held.at[(block,) + cut]
        here = src.at[cut] if src is in_ref else src.at[(block,) + cut]
        return pltpu.make_async_copy(here, there, ls.at[f, q])

    def hand_on(src, block, q):
        if not plane:
            return

        @pl.when(block // fold != c)
        def _():
            across(src, block, q).start()

        @pl.when(block // fold == c)
        def _():
            local(src, block, q).start()

    def has(lane):
        near = z + 1 - 2 * lane
        return (near >= 0) & (near < nz)

    for q in range(len(cuts)):
        for lane in (0, 1):

            @pl.when(has(lane))
            def _():
                along(in_ref, z, lane, 0, q).start()

        if plane:
            hand_on(in_ref, z, q)
        else:
            local(in_ref, z, q).start()

    def hop(dist, carry):
        for q in range(len(cuts)):
            for lane in (0, 1):
                block = z - dist * (1 - 2 * lane)

                @pl.when((block >= 0) & (block < nz))
                def _():
                    along(held, block, lane, dist - 1, q).wait_recv()

                    @pl.when(has(lane))
                    def _():
                        along(held, block, lane, dist, q).start()

                    hand_on(held, block, q)

        return carry

    lax.fori_loop(1, nz, hop, 0)

    def drain(dist, carry):
        for q in range(len(cuts)):
            for lane in (0, 1):
                block = z - dist * (1 - 2 * lane)

                @pl.when((block >= 0) & (block < nz) & has(lane))
                def _():
                    along(held, block, lane, dist, q).wait_send()

            if plane:

                @pl.when(dist // fold != c)
                def _():
                    across(held, dist, q).wait_send()

                @pl.when(dist // fold == c)
                def _():
                    local(held, dist, q).wait()

        return carry

    lax.fori_loop(0, nz, drain, 0)
    for q in range(len(cuts)):
        if not plane:
            local(in_ref, z, q).wait()
        else:
            for off in range(1, ns):
                who = lax.rem(c + off, ns)
                for f in range(fold):
                    remote(
                        place(who, f, q),
                        place(who, f, q),
                        ps.at[0, q],
                        pr.at[who, f, q],
                        {"src": who},
                    ).wait_recv()


def gather(value, nz, ns, plane, count, cid, name):
    planes, rows, width = value.shape
    fold = nz // ns
    cuts = pieces(value.shape, count)
    nq = len(cuts)
    dma = pltpu.SemaphoreType.DMA
    scratch = [dma((2, nz, nq)), dma((2, nz, nq))]
    if plane:
        out = jax.ShapeDtypeStruct((planes, ns * rows, fold * width), F32)
        scratch = [pltpu.VMEM((nz,) + value.shape, F32)] + scratch
        scratch += [dma((nz, nq)), dma((ns, fold, nq)), dma((fold, nq))]
    else:
        out = jax.ShapeDtypeStruct((nz,) + value.shape, F32)
        scratch += [dma((1, nq))]
    return pl.pallas_call(
        functools.partial(gather_kernel, nz, ns, fold, plane, cuts),
        out_shape=out,
        in_specs=[pl.BlockSpec(memory_space=pltpu.VMEM)],
        out_specs=pl.BlockSpec(memory_space=pltpu.VMEM),
        scratch_shapes=scratch,
        name=name,
        compiler_params=pltpu.CompilerParams(collective_id=cid, has_side_effects=True),
    )(value)


def bin_kernel(
    nz, cuts, groups, tables, shots, in_ref, wt_ref, out_ref, held, terms, total, order, zs, zr
):
    z = lax.axis_index("rcv")
    stencil = wt_ref.shape[0] // 2
    rows = 2 * shots
    width = in_ref.shape[-1]
    cells = nz * groups

    def has(lane):
        near = z + 1 - 2 * lane
        return (near >= 0) & (near < nz)

    barrier = pltpu.get_barrier_semaphore()
    for lane in (0, 1):

        @pl.when(has(lane))
        def _():
            pl.semaphore_signal(
                barrier, inc=1, device_id={"rcv": z + 1 - 2 * lane}, device_id_type=MESH
            )

    pl.semaphore_wait(barrier, jnp.where(z > 0, 1, 0) + jnp.where(z < nz - 1, 1, 0))

    def along(own, block, lane, dist, q):
        cut = cuts[q]
        return remote(
            in_ref.at[cut] if own else held.at[(block,) + cut],
            held.at[(block,) + cut],
            zs.at[lane, dist, q],
            zr.at[lane, dist, q],
            {"rcv": z + 1 - 2 * lane},
        )

    for q in range(len(cuts)):
        for lane in (0, 1):

            @pl.when(has(lane))
            def _():
                along(True, z, lane, 0, q).start()

    w = wt_ref[...]
    w0 = w.astype(BF16)
    rest = w - w0.astype(F32)
    w1 = rest.astype(BF16)
    w2 = (rest - w1.astype(F32)).astype(BF16)
    table_ids = lax.broadcasted_iota(jnp.int32, (tables, width), 0).astype(F32)
    cell_ids = lax.broadcasted_iota(jnp.int32, (cells, width), 0).astype(F32)

    def sums(view):
        cell = view[0, rows : rows + 1, :] * float(groups) + view[0, rows + 1 : rows + 2, :]
        table_hot = (table_ids == view[0, rows + 2 : rows + 3, :]).astype(BF16)
        picked = sum(
            jnp.dot(part, table_hot, preferred_element_type=F32) for part in (w0, w1, w2)
        )
        hot = (cell_ids == cell).astype(BF16)
        real = view[0, 0:shots, :]
        imag = view[0, shots:rows, :]
        for j in range(stencil):
            wr = picked[j : j + 1, :]
            wi = picked[stencil + j : stencil + j + 1, :]
            base = j * 2 * rows
            for part, both in enumerate((real * wr - imag * wi, real * wi + imag * wr)):
                high, low = split(both)
                at = base + part * shots
                terms[at : at + shots, :] = high
                terms[at + rows : at + rows + shots, :] = low
        found = lax.dot_general(terms[...], hot, NT, preferred_element_type=F32)
        found = found.reshape(stencil, 2, rows, cells)
        return found[:, 0] + found[:, 1]

    total[...] = sums(in_ref)

    def hop(dist, carry):
        for q in range(len(cuts)):
            for lane in (0, 1):
                block = z - dist * (1 - 2 * lane)

                @pl.when((block >= 0) & (block < nz))
                def _():
                    along(False, block, lane, dist - 1, q).wait_recv()

                    @pl.when(has(lane))
                    def _():
                        along(False, block, lane, dist, q).start()

        def add(lane, inner):
            block = z - dist * (1 - 2 * lane)

            @pl.when((block >= 0) & (block < nz))
            def _():
                total[...] += sums(held.at[block])

            return inner

        return lax.fori_loop(0, 2, add, carry)

    lax.fori_loop(1, nz, hop, 0)
    for j in range(stencil):
        order[:, j, :] = total[j].T
    out_ref[...] = order[...].reshape(cells * stencil, rows).T

    def drain(dist, carry):
        for q in range(len(cuts)):
            for lane in (0, 1):
                block = z - dist * (1 - 2 * lane)

                @pl.when((block >= 0) & (block < nz) & has(lane))
                def _():
                    along(False, block, lane, dist, q).wait_send()

        return carry

    lax.fori_loop(0, nz, drain, 0)


def bin_all(value, moveout, nz, groups, shots, cid):
    tables, stencil = moveout.shape[1:]
    width = value.shape[-1]
    weights = jnp.transpose(moveout, (0, 2, 1)).reshape(2 * stencil, tables)
    cuts = pieces(value.shape, 3)
    dma = pltpu.SemaphoreType.DMA
    vmem = pl.BlockSpec(memory_space=pltpu.VMEM)
    out = pl.pallas_call(
        functools.partial(bin_kernel, nz, cuts, groups, tables, shots),
        out_shape=jax.ShapeDtypeStruct((2 * shots, nz * groups * stencil), F32),
        in_specs=[vmem, vmem],
        out_specs=vmem,
        scratch_shapes=[
            pltpu.VMEM((nz,) + value.shape, F32),
            pltpu.VMEM((stencil * 4 * shots, width), BF16),
            pltpu.VMEM((stencil, 2 * shots, nz * groups), F32),
            pltpu.VMEM((nz * groups, stencil, 2 * shots), F32),
            dma((2, nz, len(cuts))),
            dma((2, nz, len(cuts))),
        ],
        name="bin_all",
        compiler_params=pltpu.CompilerParams(
            collective_id=cid, has_side_effects=True, vmem_limit_bytes=56 << 20
        ),
    )(value, weights)
    return out.reshape(2, shots, nz * groups * stencil)


def spread_kernel(ns, in_ref, out_ref, ss, rs, ls):
    c = lax.axis_index("src")
    rows = in_ref.shape[1]
    width = out_ref.shape[2]
    barrier = pltpu.get_barrier_semaphore()
    for off in range(1, ns):
        pl.semaphore_signal(
            barrier, inc=1, device_id={"src": lax.rem(c + off, ns)}, device_id_type=MESH
        )
    pl.semaphore_wait(barrier, ns - 1)

    def part(who, p):
        return in_ref.at[p, :, pl.ds(pl.multiple_of(who * width, 128), width)]

    def place(who, p):
        return out_ref.at[p, pl.ds(pl.multiple_of(who * rows, 8), rows), :]

    sends = []
    for off in range(1, ns):
        for p in (0, 1):
            who = lax.rem(c + off, ns)
            copy = remote(
                part(who, p), place(c, p), ss.at[off - 1, p], rs.at[off - 1, p], {"src": who}
            )
            copy.start()
            sends.append(copy)
    own = [pltpu.make_async_copy(part(c, p), place(c, p), ls.at[p]) for p in (0, 1)]
    for copy in own:
        copy.start()
    for copy in own:
        copy.wait()
    for off in range(1, ns):
        for p in (0, 1):
            who = lax.rem(c + ns - off, ns)
            remote(
                place(who, p), place(who, p), ss.at[off - 1, p], rs.at[off - 1, p], {"src": who}
            ).wait_recv()
    for copy in sends:
        copy.wait_send()


def spread(value, ns, cid):
    _, rows, width = value.shape
    dma = pltpu.SemaphoreType.DMA
    vmem = pl.BlockSpec(memory_space=pltpu.VMEM)
    return pl.pallas_call(
        functools.partial(spread_kernel, ns),
        out_shape=jax.ShapeDtypeStruct((2, ns * rows, width // ns), F32),
        in_specs=[vmem],
        out_specs=vmem,
        scratch_shapes=[dma((ns - 1, 2)), dma((ns - 1, 2)), dma((2,))],
        name="spread",
        compiler_params=pltpu.CompilerParams(collective_id=cid, has_side_effects=True),
    )(value)


def multiply_kernel(
    ns, shots, steps, p_ref, a_ref, out_ref, high, low, mine, give, take, pass_on, got, s1, r1, s2, r2
):
    step = pl.program_id(0)
    c = lax.axis_index("src")
    core = lax.rem(c, 2)
    chip = c // 2
    chips = ns // 2
    half = ns * shots
    tile = a_ref.shape[1]

    @pl.when(step == 0)
    def _():
        barrier = pltpu.get_barrier_semaphore()
        pl.semaphore_signal(barrier, inc=1, device_id={"src": c + 1 - 2 * core}, device_id_type=MESH)
        for off in range(1, chips):
            who = 2 * lax.rem(chip + off, chips) + core
            pl.semaphore_signal(barrier, inc=1, device_id={"src": who}, device_id_type=MESH)
        for part in (0, 1):
            top, rest = split(p_ref[part])
            high[part * half : (part + 1) * half, :] = top
            low[part * half : (part + 1) * half, :] = rest
        pl.semaphore_wait(barrier, chips)

    def to_partner(at):
        return remote(give.at[at], take.at[at], s1.at[at], r1.at[at], {"src": c + 1 - 2 * core})

    def to_chip(at, off):
        who = 2 * lax.rem(chip + off, chips) + core
        return remote(
            pass_on.at[at, off - 1],
            got.at[at, off - 1],
            s2.at[at, off - 1],
            r2.at[at, off - 1],
            {"src": who},
        )

    def reduce_pair(at):
        to_partner(at).wait_recv()
        for off in range(1, chips):
            there = lax.rem(chip + off, chips)
            pass_on[at, off - 1] = mine[at, there] + take[at, there]
            to_chip(at, off).start()
        mine[at, chip] += take[at, chip]

    def times(part):
        top, rest = split(a_ref[part])
        total = lax.dot_general(high[...], top, NT, preferred_element_type=F32)
        total += lax.dot_general(low[...], top, NT, preferred_element_type=F32)
        total += lax.dot_general(high[...], rest, NT, preferred_element_type=F32)
        return total

    by_real = times(0)
    by_imag = times(1)
    both = (by_real[:half] - by_imag[half:], by_imag[:half] + by_real[half:])
    for part in (0, 1):
        for who in range(ns):
            value = both[part][who * shots : (who + 1) * shots]

            @pl.when(core == who % 2)
            def _():
                mine[step, who // 2, part] = value

            @pl.when(core != who % 2)
            def _():
                give[step, who // 2, part] = value

    to_partner(step).start()

    @pl.when(step > 0)
    def _():
        reduce_pair(step - 1)

    @pl.when(step == steps - 1)
    def _():
        reduce_pair(step)
        for at in range(steps):
            total = mine[at, chip]
            for off in range(1, chips):
                to_chip(at, off).wait_recv()
                total += got[at, off - 1]
            out_ref[:, :, at * tile : (at + 1) * tile] = total
        for at in range(steps):
            to_partner(at).wait_send()
            for off in range(1, chips):
                to_chip(at, off).wait_send()


def multiply(columns, aperture, ns, cid):
    _, half, depth = columns.shape
    outs = aperture.shape[1]
    shots = half // ns
    tile = min(outs, 256)
    steps = outs // tile
    chips = ns // 2
    dma = pltpu.SemaphoreType.DMA
    block = (2, shots, tile)
    return pl.pallas_call(
        functools.partial(multiply_kernel, ns, shots, steps),
        grid=(steps,),
        out_shape=jax.ShapeDtypeStruct((2, shots, outs), F32),
        in_specs=[
            pl.BlockSpec(memory_space=pltpu.VMEM),
            pl.BlockSpec((2, tile, depth), lambda i: (0, i, 0)),
        ],
        out_specs=pl.BlockSpec(memory_space=pltpu.VMEM),
        scratch_shapes=[
            pltpu.VMEM((2 * half, depth), BF16),
            pltpu.VMEM((2 * half, depth), BF16),
            pltpu.VMEM((steps, chips) + block, F32),
            pltpu.VMEM((steps, chips) + block, F32),
            pltpu.VMEM((steps, chips) + block, F32),
            pltpu.VMEM((steps, chips - 1) + block, F32),
            pltpu.VMEM((steps, chips - 1) + block, F32),
            dma((steps,)),
            dma((steps,)),
            dma((steps, chips - 1)),
            dma((steps, chips - 1)),
        ],
        name="multiply",
        compiler_params=pltpu.CompilerParams(
            collective_id=cid,
            has_side_effects=True,
            dimension_semantics=("arbitrary",),
            vmem_limit_bytes=56 << 20,
        ),
    )(columns, aperture)


def per_device(nz, ns, traces, moveout, owner, group, table, aperture, shaping):
    groups = aperture.shape[1] // moveout.shape[2]
    shots = traces.shape[0]
    width = traces.shape[2]
    codes = jnp.stack([owner, group, table]).astype(F32)
    codes = jnp.concatenate([codes, jnp.zeros((5, width), F32)])
    flat = jnp.transpose(traces, (1, 0, 2)).reshape(2 * shots, width)
    everyone = bin_all(jnp.concatenate([flat, codes])[None], moveout, nz, groups, shots, 0)
    bins = aperture.shape[1]
    binned = lax.dynamic_slice_in_dim(everyone, lax.axis_index("rcv") * bins, bins, 2)
    form = jnp.transpose(shaping, (1, 0, 2))
    panel = binned
    for sweep in range(ITERS):
        if sweep == 0:
            columns = spread(everyone, ns, 3)
        else:
            columns = gather(panel, nz, ns, True, 8, 1, "gather_panel")
        found = multiply(columns, aperture, ns, 2)
        panel = jnp.stack(
            [
                binned[0] - (form[0] * found[0] - form[1] * found[1]),
                binned[1] - (form[0] * found[1] + form[1] * found[0]),
            ]
        )
    return jnp.transpose(panel, (1, 0, 2))


def solution(mesh):
    nz, ns = mesh.shape["rcv"], mesh.shape["src"]
    in_specs = (
        P(("freq", "src"), None, "rcv"),
        P(None, "freq", None),
        P(("freq", "rcv")),
        P(("freq", "rcv")),
        P(("freq", "rcv")),
        P(None, ("freq", "rcv"), "src"),
        P(("freq", "src"), None, "rcv"),
    )
    out_specs = P(("freq", "src"), None, "rcv")
    return jax.shard_map(
        functools.partial(per_device, nz, ns),
        mesh=mesh,
        in_specs=in_specs,
        out_specs=out_specs,
        check_vma=False,
    )
```
